1024 devices in a mesh: load: 2 (over z_lo), sy: 64 (over y, x), sz: 8 (over z_hi, core).
Axes of the slice: x: 8, y: 8, z: 8 (z_hi: 4, z_lo: 2; z = z_hi * 2 + z_lo), core: 2. Of those that a mesh axis runs over, the one named last changes fastest.
Arguments:
- displacements: float32 [4, 3, 32, 1024, 512], P('load', None, 'sz', 'sy'), may hold values from -2.4 to 2.4
- density: float32 [32, 1024, 512], P('sz', 'sy'), may hold values from 0.05 to 1
- solid: int32 [32, 1024, 512], P('sz', 'sy'), may hold values 0 or 1
- fixed: int32 [32, 1024, 512], P('sz', 'sy'), may hold values 0 or 1
Outputs:
- sensitivity: float32 [32, 1024, 512], P('sz', 'sy')
The draws below stay inside these ranges and needn't reach their ends.
All inputs are finite; a program needn't handle non-finite values. No bound on the sum of `solid` or of `fixed` on one device may be relied on, other than what follows from the above.
Results may differ from the reference program's by a relative error of at most 0.0001.
Values sent between devices are 32-bit elements; how exact they have to be, the bound alone decides.
A program may use at most 32 MiB of HBM per device.

```python
import math
import jax
import jax.numpy as jnp
import numpy as np
from jax import lax

NX = 512
LOADS = 4
NY = 1024
NZ = 32


def with_ends(drawn, rng, least, high):
    extent = drawn.shape
    spot = [jax.random.randint(jax.random.fold_in(rng, axis), (), 0, extent[axis]) for axis in range(len(extent))]
    drawn = drawn.at[tuple(spot)].set(least)
    longest = extent.index(max(extent))
    spot[longest] = (spot[longest] + 1) % extent[longest]
    return drawn.at[tuple(spot)].set(high)


def shard_levels(stream_key, dims, shards, least, high):
    level = 1.0
    for dim, blocks in shards:
        draws = jax.random.uniform(jax.random.fold_in(jax.random.fold_in(stream_key, 6), dim), (blocks,), jnp.float32, least / len(shards), high / len(shards))
        level = level * jnp.repeat(jnp.exp(draws), dims[dim] // blocks).reshape((-1,) + (1,) * (len(dims) - 1 - dim))
    return level


def gaussian(stream_key, extent, deviation, reach, shards=(), kind=jnp.bfloat16):
    values = jax.random.normal(stream_key, extent, jnp.float32) * deviation
    if len(shards) > 0:
        values = shard_levels(stream_key, extent, shards, -0.22, 0.18) * values
    return jnp.clip(values, min=-reach, max=reach).astype(kind)


def setup_inputs(seed: int = 0) -> dict:
    arg_keys = jax.random.split(jax.random.key(seed), 5)
    displacements = gaussian(arg_keys[0], (LOADS, 3, NZ, NY, NX), 0.3, 2.4, ((0, 2), (2, 8), (3, 64)), jnp.float32)
    density = jnp.clip(jnp.exp(math.log(1.0) - 2.9957323 * jax.random.uniform(arg_keys[1], (NZ, NY, NX), jnp.float32) ** shard_levels(arg_keys[1], (NZ, NY, NX), ((0, 8), (1, 64)), -0.2, 0.2)), 0.05, 1.0)
    solid = with_ends((jax.random.randint(arg_keys[2], (NZ, NY, NX), 0, 4) < 3).astype(jnp.int32), jax.random.fold_in(arg_keys[2], 1), 0, 1)
    fixed = with_ends((jax.random.randint(arg_keys[3], (NZ, NY, NX), 0, 8) < 1).astype(jnp.int32), jax.random.fold_in(arg_keys[3], 1), 0, 1)
    return dict(displacements=displacements, density=density, solid=solid, fixed=fixed)


def element_matrix():
    corners = np.array([[-1.0, -1.0, -1.0], [1.0, -1.0, -1.0], [1.0, 1.0, -1.0], [-1.0, 1.0, -1.0], [-1.0, -1.0, 1.0], [1.0, -1.0, 1.0], [1.0, 1.0, 1.0], [-1.0, 1.0, 1.0]])
    poisson = 0.3
    lame = poisson / ((1.0 + poisson) * (1.0 - 2.0 * poisson))
    shear = 1.0 / (2.0 * (1.0 + poisson))
    elastic = np.zeros((6, 6))
    elastic[:3, :3] = lame
    for k in range(3):
        elastic[k, k] += 2.0 * shear
        elastic[3 + k, 3 + k] = shear
    gauss = 1.0 / np.sqrt(3.0)
    stiffness = np.zeros((24, 24))
    for gi in range(2):
        for gj in range(2):
            for gk in range(2):
                point = np.array([(2 * gi - 1) * gauss, (2 * gj - 1) * gauss, (2 * gk - 1) * gauss])
                strain = np.zeros((6, 24))
                for node in range(8):
                    grads = np.zeros(3)
                    for k in range(3):
                        value = corners[node, k] / 8.0
                        for m in range(3):
                            if m != k:
                                value = value * (1.0 + point[m] * corners[node, m])
                        grads[k] = 2.0 * value
                    col = 3 * node
                    strain[0, col] = grads[0]
                    strain[1, col + 1] = grads[1]
                    strain[2, col + 2] = grads[2]
                    strain[3, col] = grads[1]
                    strain[3, col + 1] = grads[0]
                    strain[4, col + 1] = grads[2]
                    strain[4, col + 2] = grads[1]
                    strain[5, col] = grads[2]
                    strain[5, col + 2] = grads[0]
                stiffness += strain.T @ elastic @ strain / 8.0
    return stiffness
OFFSETS = [(0, 0, 0), (1, 0, 0), (1, 1, 0), (0, 1, 0), (0, 0, 1), (1, 0, 1), (1, 1, 1), (0, 1, 1)]

def weight_line(coord, count):
    total = jnp.zeros(coord.shape, jnp.float32)
    for step in range(-3, 4):
        inside = (coord + step >= 0) & (coord + step < count)
        total = total + jnp.where(inside, 4.0 - abs(step), 0.0).astype(jnp.float32)
    return total

def spread_axis(padded, axis, length):
    total = None
    for k in range(7):
        piece = (4.0 - abs(k - 3)) * lax.slice_in_dim(padded, k, k + length, axis=axis)
        total = piece if total is None else total + piece
    return total

def reference(displacements, density, solid, fixed):
    stiffness = jnp.asarray(element_matrix(), jnp.float32)
    held = displacements * (1 - fixed).astype(jnp.float32)[None, None]
    padded = jnp.pad(held, ((0, 0), (0, 0), (0, 1), (0, 1), (0, 1)))

    def slab_energy(zidx):
        block = lax.dynamic_slice_in_dim(padded, zidx, 2, axis=2)
        nodes = [block[:, :, c, b:b + NY, a:a + NX] for a, b, c in OFFSETS]
        local = jnp.stack(nodes, axis=1).reshape(LOADS, 24, NY * NX)
        image = jnp.einsum('ij,ljc->lic', stiffness, local, precision=lax.Precision.HIGHEST)
        return lax.optimization_barrier(jnp.sum(local * image, axis=(0, 1))).reshape(NY, NX)
    energy = lax.map(slab_energy, jnp.arange(NZ, dtype=jnp.int32))
    term = solid.astype(jnp.float32) * (-3.0 * density * density) * energy
    hz = weight_line(jnp.arange(NZ, dtype=jnp.int32), NZ)
    hy = weight_line(jnp.arange(NY, dtype=jnp.int32), NY)
    hx = weight_line(jnp.arange(NX, dtype=jnp.int32), NX)
    quotient = term / (hz[:, None, None] * hy[None, :, None] * hx[None, None, :])
    padq = jnp.pad(quotient, 3)
    result = spread_axis(padq, 2, NX)
    result = spread_axis(result, 1, NY)
    result = spread_axis(result, 0, NZ)
    return result
```

```python
import functools

import jax
import jax.numpy as jnp
from jax import lax
from jax.experimental import pallas as pl
from jax.experimental.pallas import tpu as pltpu
from jax.sharding import PartitionSpec as P

MESH = pl.DeviceIdType.MESH
F32 = jnp.float32
LAME = 0.3 / (1.3 * 0.4)
SHEAR = 1.0 / 2.6
CHUNK = 128


def line_weight(coord, count):
    total = None
    for step in range(-3, 4):
        inside = (coord + step >= 0) & (coord + step < count)
        piece = jnp.where(inside, F32(4.0 - abs(step)), F32(0.0))
        total = piece if total is None else total + piece
    return total


def box_twice(value, axis):
    size = value.shape[axis]
    value = value + pltpu.roll(value, size - 1, axis)
    value = value + pltpu.roll(value, size - 2, axis)
    value = value + pltpu.roll(value, 1, axis)
    return value + pltpu.roll(value, 2, axis)


def filter_x(value):
    rows, cols = value.shape
    padded = jnp.concatenate([value, jnp.zeros((rows, 128), F32)], axis=1)
    return box_twice(padded, 1)[:, :cols]


def filter_z(layers):
    pairs = [layers[k] + layers[k + 1] for k in range(9)]
    runs = [pairs[k] + pairs[k + 2] for k in range(7)]
    pairs = [runs[k] + runs[k + 1] for k in range(6)]
    return [pairs[k] + pairs[k + 2] for k in range(4)]


def mode_energy(low, high):
    x, y, z = range(3)
    mode = []
    for k in range(3):
        (ls, lx, ly, lxy), (hs, hx, hy, hxy) = low[k], high[k]
        mode.append(
            dict(
                z=hs - ls, x=hx + lx, y=hy + ly, xy=hxy + lxy,
                xz=hx - lx, yz=hy - ly, xyz=hxy - lxy,
            )
        )
    sq = lambda v: v * v
    a, b, c = mode
    div = sq(a["x"] + b["y"] + c["z"])
    normal = sq(a["x"]) + sq(b["y"]) + sq(c["z"])
    shear = sq(a["y"] + b["x"]) + sq(b["z"] + c["y"]) + sq(a["z"] + c["x"])
    bend = sq(b["xy"] + c["xz"]) + sq(a["xy"] + c["yz"]) + sq(a["xz"] + b["yz"])
    six = (
        sq(a["xy"]) + sq(a["xz"]) + sq(b["xy"]) + sq(b["yz"]) + sq(c["xz"]) + sq(c["yz"])
    )
    twist = sq(a["yz"] + b["xz"]) + sq(a["yz"] + c["xy"]) + sq(b["xz"] + c["xy"])
    last = sq(a["xyz"]) + sq(b["xyz"]) + sq(c["xyz"])
    return div, normal, shear, bend, six, twist, last


def weigh(groups):
    div, normal, shear, bend, six, twist, last = groups
    s = 1.0 / 16.0
    return (
        F32(s * LAME) * div
        + F32(s * 2.0 * SHEAR) * normal
        + F32(s * SHEAR) * (shear + six)
        + F32(s * LAME / 3.0) * bend
        + F32(s * SHEAR / 3.0) * twist
        + F32(s * (LAME + 4.0 * SHEAR) / 9.0) * last
    )


def kernel(
    disp, dens, solid, fixed, out,
    raw, den, sol, fix, held, faces, energy, coef, part, other, ext,
    load_sem, send, recv, ready,
):
    nsz, nsy, nload = lax.axis_size("sz"), lax.axis_size("sy"), lax.axis_size("load")
    sz, sy, ld = lax.axis_index("sz"), lax.axis_index("sy"), lax.axis_index("load")
    up, down = lax.rem(sz + 1, nsz), lax.rem(sz + nsz - 1, nsz)
    right, left = lax.rem(sy + 1, nsy), lax.rem(sy + nsy - 1, nsy)
    mate = lax.rem(ld + 1, nload)

    loads = [
        pltpu.make_async_copy(s, d, load_sem.at[k])
        for k, (s, d) in enumerate(((disp, raw), (fixed, fix), (dens, den), (solid, sol)))
    ]
    for copy in loads:
        copy.start()
    barrier = pltpu.get_barrier_semaphore()
    around = ({"sz": up}, {"sz": down}, {"sy": right}, {"sy": left}, {"load": mate})
    for device in around:
        pl.semaphore_signal(barrier, inc=1, device_id=device, device_id_type=MESH)

    ext[:, 19:21, :] = jnp.zeros((10, 2, 512), F32)
    loads[0].wait()
    loads[1].wait()

    def hold(z, carry):
        free = F32(1.0) - fix[z].astype(F32)
        for case in range(2):
            for k in range(3):
                held[3 * case + k, z, 0:16, :] = raw[case, k, z] * free
        return carry

    lax.fori_loop(0, 4, hold, 0)
    pl.semaphore_wait(barrier, 5)

    started = []

    def send_to(k, src, dst, device):
        copy = pltpu.make_async_remote_copy(
            src_ref=src, dst_ref=dst, send_sem=send.at[k], recv_sem=recv.at[k],
            device_id=device, device_id_type=MESH,
        )
        copy.start()
        started.append(copy)
        return copy

    node_y = send_to(0, held.at[:, 0:4, 0:1], held.at[:, 0:4, 16:17], {"sy": left})
    node_z = send_to(1, held.at[:, 0, 0:16], held.at[:, 4, 0:16], {"sz": down})
    for device in around[:2]:
        pl.semaphore_signal(ready, inc=1, device_id=device, device_id_type=MESH)

    loads[2].wait()
    loads[3].wait()
    row = lax.broadcasted_iota(jnp.int32, (16, 512), 0)
    lane = lax.broadcasted_iota(jnp.int32, (16, 512), 1)
    area = line_weight(lane, 512) * line_weight(row + sy * 16, nsy * 16)
    for z in range(4):
        weight = area * line_weight(sz * 4 + z, nsz * 4)
        d = den[z]
        coef[z] = sol[z].astype(F32) * (F32(-3.0) * d * d) / weight

    last_lane = lax.broadcasted_iota(jnp.int32, (8, 512), 1) == 511

    def next_x(value):
        return jnp.where(last_lane, F32(0.0), pltpu.roll(value, 511, 1))

    def make_faces(half, z):
        r = 8 * half
        for k in range(6):
            near = held[k, z, r : r + 8, :]
            far = held[k, z, r + 1 : r + 9, :]
            total, diff = near + far, far - near
            total_x, diff_x = next_x(total), next_x(diff)
            faces[half, z, 4 * k] = total_x + total
            faces[half, z, 4 * k + 1] = total_x - total
            faces[half, z, 4 * k + 2] = diff_x + diff
            faces[half, z, 4 * k + 3] = diff_x - diff

    def faces_loop(half, first, last):
        def step(z, carry):
            make_faces(half, z)
            return carry

        lax.fori_loop(first, last, step, 0)

    def energy_loop(half, first, last):
        def step(i, carry):
            z, j = first + i // 4, i % 4
            cols = pl.ds(pl.multiple_of(j * CHUNK, CHUNK), CHUNK)
            groups = None
            for case in range(2):
                sides = [
                    [
                        [faces[half, zz, 12 * case + 4 * k + m, :, cols] for m in range(4)]
                        for k in range(3)
                    ]
                    for zz in (z, z + 1)
                ]
                got = mode_energy(*sides)
                groups = got if groups is None else [p + q for p, q in zip(groups, got)]
            energy[z, 8 * half : 8 * half + 8, cols] = weigh(groups)
            return carry

        lax.fori_loop(0, 4 * (last - first), step, 0)

    def finish_layer(z):
        part[z] = filter_x(energy[z] * coef[z])

    faces_loop(0, 0, 4)
    energy_loop(0, 0, 3)
    node_y.wait_recv()

    @pl.when(sy == nsy - 1)
    def _():
        held[:, 0:4, 16:17, :] = jnp.zeros((6, 4, 1, 512), F32)

    node_c = send_to(2, held.at[:, 0, 16:17], held.at[:, 4, 16:17], {"sz": down})
    faces_loop(1, 0, 4)
    energy_loop(1, 0, 3)
    for z in range(3):
        finish_layer(z)
    pair_a = send_to(3, part.at[0:3], other.at[0:3], {"load": mate})
    node_z.wait_recv()

    @pl.when(sz == nsz - 1)
    def _():
        held[:, 4, 0:16, :] = jnp.zeros((6, 16, 512), F32)

    faces_loop(0, 4, 5)
    energy_loop(0, 3, 4)
    node_c.wait_recv()

    @pl.when((sy == nsy - 1) | (sz == nsz - 1))
    def _():
        held[:, 4, 16:17, :] = jnp.zeros((6, 1, 512), F32)

    faces_loop(1, 4, 5)
    energy_loop(1, 3, 4)
    finish_layer(3)
    pair_b = send_to(4, part.at[3:4], other.at[3:4], {"load": mate})

    pl.semaphore_wait(ready, 2)
    pair_a.wait_recv()
    for z in range(3):
        ext[3 + z, 0:16, :] = part[z] + other[z]
    halo = [
        send_to(5, ext.at[3:6, 0:16], ext.at[7:10, 0:16], {"sz": down}),
        send_to(6, ext.at[3:6, 0:3], ext.at[7:10, 16:19], {"sz": down, "sy": left}),
        send_to(7, ext.at[3:6, 13:16], ext.at[7:10, 21:24], {"sz": down, "sy": right}),
    ]
    pair_b.wait_recv()
    ext[6, 0:16, :] = part[3] + other[3]
    halo += [
        send_to(8, ext.at[4:7, 0:16], ext.at[0:3, 0:16], {"sz": up}),
        send_to(9, ext.at[4:7, 0:3], ext.at[0:3, 16:19], {"sz": up, "sy": left}),
        send_to(10, ext.at[4:7, 13:16], ext.at[0:3, 21:24], {"sz": up, "sy": right}),
        send_to(11, ext.at[3:7, 0:3], ext.at[3:7, 16:19], {"sy": left}),
        send_to(12, ext.at[3:7, 13:16], ext.at[3:7, 21:24], {"sy": right}),
    ]
    for copy in halo:
        copy.wait_recv()

    @pl.when(sz == nsz - 1)
    def _():
        ext[7:10] = jnp.zeros((3, 24, 512), F32)

    @pl.when(sz == 0)
    def _():
        ext[0:3] = jnp.zeros((3, 24, 512), F32)

    @pl.when(sy == nsy - 1)
    def _():
        ext[:, 16:19, :] = jnp.zeros((10, 3, 512), F32)

    @pl.when(sy == 0)
    def _():
        ext[:, 21:24, :] = jnp.zeros((10, 3, 512), F32)

    for j in range(4):
        cols = slice(j * CHUNK, (j + 1) * CHUNK)
        layers = filter_z([ext[k, :, cols] for k in range(10)])
        for z in range(4):
            out[z, :, cols] = box_twice(layers[z], 0)[0:16]
    for copy in started:
        copy.wait_send()


def body(displacements, density, solid, fixed):
    dma = pltpu.SemaphoreType.DMA
    return pl.pallas_call(
        kernel,
        out_shape=jax.ShapeDtypeStruct((4, 16, 512), F32),
        in_specs=[pl.BlockSpec(memory_space=pl.ANY)] * 4,
        out_specs=pl.BlockSpec(memory_space=pltpu.VMEM),
        scratch_shapes=[
            pltpu.VMEM((2, 3, 4, 16, 512), F32),
            pltpu.VMEM((4, 16, 512), F32),
            pltpu.VMEM((4, 16, 512), jnp.int32),
            pltpu.VMEM((4, 16, 512), jnp.int32),
            pltpu.VMEM((6, 5, 24, 512), F32),
            pltpu.VMEM((2, 5, 24, 8, 512), F32),
            pltpu.VMEM((4, 16, 512), F32),
            pltpu.VMEM((4, 16, 512), F32),
            pltpu.VMEM((4, 16, 512), F32),
            pltpu.VMEM((4, 16, 512), F32),
            pltpu.VMEM((10, 24, 512), F32),
            dma((4,)),
            dma((13,)),
            dma((13,)),
            pltpu.SemaphoreType.REGULAR,
        ],
        compiler_params=pltpu.CompilerParams(collective_id=0, has_side_effects=True),
    )(displacements, density, solid, fixed)


def solution(mesh):
    return jax.shard_map(
        body,
        mesh=mesh,
        in_specs=(
            P("load", None, "sz", "sy", None),
            P("sz", "sy", None),
            P("sz", "sy", None),
            P("sz", "sy", None),
        ),
        out_specs=P("sz", "sy", None),
        check_vma=False,
    )
```

```python
import functools

import jax
import jax.numpy as jnp
from jax import lax
from jax.experimental import pallas as pl
from jax.experimental.pallas import tpu as pltpu
from jax.sharding import PartitionSpec as P

MESH = pl.DeviceIdType.MESH
F32 = jnp.float32
LAME = 0.3 / (1.3 * 0.4)
SHEAR = 1.0 / 2.6
CHUNK = 128


def line_weight(coord, count):
    total = None
    for step in range(-3, 4):
        inside = (coord + step >= 0) & (coord + step < count)
        piece = jnp.where(inside, F32(4.0 - abs(step)), F32(0.0))
        total = piece if total is None else total + piece
    return total


def box_twice(value, axis):
    size = value.shape[axis]
    value = value + pltpu.roll(value, size - 1, axis)
    value = value + pltpu.roll(value, size - 2, axis)
    value = value + pltpu.roll(value, 1, axis)
    return value + pltpu.roll(value, 2, axis)


def filter_x(value):
    rows, cols = value.shape
    padded = jnp.concatenate([value, jnp.zeros((rows, 128), F32)], axis=1)
    return box_twice(padded, 1)[:, :cols]


def filter_z(layers):
    pairs = [layers[k] + layers[k + 1] for k in range(9)]
    runs = [pairs[k] + pairs[k + 2] for k in range(7)]
    pairs = [runs[k] + runs[k + 1] for k in range(6)]
    return [pairs[k] + pairs[k + 2] for k in range(4)]


def mode_energy(low, high):
    x, y, z = range(3)
    mode = []
    for k in range(3):
        (ls, lx, ly, lxy), (hs, hx, hy, hxy) = low[k], high[k]
        mode.append(
            dict(
                z=hs - ls, x=hx + lx, y=hy + ly, xy=hxy + lxy,
                xz=hx - lx, yz=hy - ly, xyz=hxy - lxy,
            )
        )
    sq = lambda v: v * v
    a, b, c = mode
    div = sq(a["x"] + b["y"] + c["z"])
    normal = sq(a["x"]) + sq(b["y"]) + sq(c["z"])
    shear = sq(a["y"] + b["x"]) + sq(b["z"] + c["y"]) + sq(a["z"] + c["x"])
    bend = sq(b["xy"] + c["xz"]) + sq(a["xy"] + c["yz"]) + sq(a["xz"] + b["yz"])
    six = (
        sq(a["xy"]) + sq(a["xz"]) + sq(b["xy"]) + sq(b["yz"]) + sq(c["xz"]) + sq(c["yz"])
    )
    twist = sq(a["yz"] + b["xz"]) + sq(a["yz"] + c["xy"]) + sq(b["xz"] + c["xy"])
    last = sq(a["xyz"]) + sq(b["xyz"]) + sq(c["xyz"])
    return div, normal, shear, bend, six, twist, last


def weigh(groups):
    div, normal, shear, bend, six, twist, last = groups
    s = 1.0 / 16.0
    return (
        F32(s * LAME) * div
        + F32(s * 2.0 * SHEAR) * normal
        + F32(s * SHEAR) * (shear + six)
        + F32(s * LAME / 3.0) * bend
        + F32(s * SHEAR / 3.0) * twist
        + F32(s * (LAME + 4.0 * SHEAR) / 9.0) * last
    )


def kernel(
    disp, dens, solid, fixed, out,
    raw, den, sol, fix, held, faces, energy, coef, part, other, ext,
    load_sem, send, recv, ready,
):
    nsz, nsy, nload = lax.axis_size("sz"), lax.axis_size("sy"), lax.axis_size("load")
    sz, sy, ld = lax.axis_index("sz"), lax.axis_index("sy"), lax.axis_index("load")
    has_up, has_down, has_right, has_left = sz < nsz - 1, sz > 0, sy < nsy - 1, sy > 0
    up, down, right, left = {"sz": sz + 1}, {"sz": sz - 1}, {"sy": sy + 1}, {"sy": sy - 1}
    mate = {"load": lax.rem(ld + 1, nload)}

    loads = [
        pltpu.make_async_copy(s, d, load_sem.at[k])
        for k, (s, d) in enumerate(((disp, raw), (fixed, fix), (dens, den), (solid, sol)))
    ]
    for copy in loads:
        copy.start()
    barrier = pltpu.get_barrier_semaphore()

    def greet(sem, device, when=None):
        if when is None:
            pl.semaphore_signal(sem, inc=1, device_id=device, device_id_type=MESH)
        else:
            pl.when(when)(lambda: greet(sem, device))

    greet(barrier, mate)
    greet(barrier, right, has_right)
    greet(barrier, up, has_up)

    ext[:, 19:21, :] = jnp.zeros((10, 2, 512), F32)

    @pl.when(jnp.logical_not(has_up))
    def _():
        ext[7:10] = jnp.zeros((3, 24, 512), F32)
        held[:, 4] = jnp.zeros((6, 24, 512), F32)

    @pl.when(jnp.logical_not(has_down))
    def _():
        ext[0:3] = jnp.zeros((3, 24, 512), F32)

    @pl.when(jnp.logical_not(has_right))
    def _():
        ext[:, 16:19, :] = jnp.zeros((10, 3, 512), F32)
        held[:, :, 16:17, :] = jnp.zeros((6, 5, 1, 512), F32)

    @pl.when(jnp.logical_not(has_left))
    def _():
        ext[:, 21:24, :] = jnp.zeros((10, 3, 512), F32)

    loads[0].wait()
    loads[1].wait()

    def hold(z, carry):
        free = F32(1.0) - fix[z].astype(F32)
        for case in range(2):
            for k in range(3):
                held[3 * case + k, z, 0:16, :] = raw[case, k, z] * free
        return carry

    lax.fori_loop(0, 4, hold, 0)
    pl.semaphore_wait(barrier, 1 + has_down.astype(jnp.int32) + has_left.astype(jnp.int32))

    started = []

    def send_to(k, src, dst, device, sends=None, takes=None):
        copy = pltpu.make_async_remote_copy(
            src_ref=src, dst_ref=dst, send_sem=send.at[k], recv_sem=recv.at[k],
            device_id=device, device_id_type=MESH,
        )

        def each(act, when):
            if when is None:
                act()
            else:
                pl.when(when)(act)

        each(copy.start, sends)
        started.append(lambda: each(copy.wait_send, sends))
        return lambda: each(copy.wait_recv, takes)

    node_z = send_to(1, held.at[:, 0, 0:16], held.at[:, 4, 0:16], down, has_down, has_up)
    node_y = send_to(0, held.at[:, 0:4, 0:1], held.at[:, 0:4, 16:17], left, has_left, has_right)

    loads[2].wait()
    loads[3].wait()
    row = lax.broadcasted_iota(jnp.int32, (16, 512), 0)
    lane = lax.broadcasted_iota(jnp.int32, (16, 512), 1)
    area = line_weight(lane, 512) * line_weight(row + sy * 16, nsy * 16)
    for z in range(4):
        weight = area * line_weight(sz * 4 + z, nsz * 4)
        d = den[z]
        coef[z] = sol[z].astype(F32) * (F32(-3.0) * d * d) / weight

    last_lane = lax.broadcasted_iota(jnp.int32, (8, 512), 1) == 511

    def next_x(value):
        return jnp.where(last_lane, F32(0.0), pltpu.roll(value, 511, 1))

    def make_faces(half, z):
        r = 8 * half
        for k in range(6):
            near = held[k, z, r : r + 8, :]
            far = held[k, z, r + 1 : r + 9, :]
            total, diff = near + far, far - near
            total_x, diff_x = next_x(total), next_x(diff)
            faces[half, z, 4 * k] = total_x + total
            faces[half, z, 4 * k + 1] = total_x - total
            faces[half, z, 4 * k + 2] = diff_x + diff
            faces[half, z, 4 * k + 3] = diff_x - diff

    def faces_loop(half, first, last):
        def step(z, carry):
            make_faces(half, z)
            return carry

        lax.fori_loop(first, last, step, 0)

    def energy_loop(half, first, last):
        def step(i, carry):
            z, j = first + i // 4, i % 4
            cols = pl.ds(pl.multiple_of(j * CHUNK, CHUNK), CHUNK)
            groups = None
            for case in range(2):
                sides = [
                    [
                        [faces[half, zz, 12 * case + 4 * k + m, :, cols] for m in range(4)]
                        for k in range(3)
                    ]
                    for zz in (z, z + 1)
                ]
                got = mode_energy(*sides)
                groups = got if groups is None else [p + q for p, q in zip(groups, got)]
            energy[z, 8 * half : 8 * half + 8, cols] = weigh(groups)
            return carry

        lax.fori_loop(0, 4 * (last - first), step, 0)

    def finish_layer(z):
        part[z] = filter_x(energy[z] * coef[z])

    faces_loop(0, 0, 4)
    energy_loop(0, 0, 3)
    node_y()
    greet(ready, right, has_right)
    node_c = send_to(
        2, held.at[:, 0, 16:17], held.at[:, 4, 16:17], down, has_down & has_right, has_up & has_right
    )
    faces_loop(1, 0, 4)
    energy_loop(1, 0, 3)
    for z in range(3):
        finish_layer(z)
    pair_a = send_to(3, part.at[0:3], other.at[0:3], mate)
    node_z()
    faces_loop(0, 4, 5)
    energy_loop(0, 3, 4)
    node_c()
    faces_loop(1, 4, 5)
    energy_loop(1, 3, 4)
    finish_layer(3)
    pair_b = send_to(4, part.at[3:4], other.at[3:4], mate)

    @pl.when(has_left)
    def _():
        pl.semaphore_wait(ready, 1)

    pair_a()
    for z in range(3):
        ext[3 + z, 0:16, :] = part[z] + other[z]
    halo = [send_to(5, ext.at[3:6, 0:16], ext.at[7:10, 0:16], down, has_down, has_up)]
    pair_b()
    ext[6, 0:16, :] = part[3] + other[3]
    halo += [
        send_to(6, ext.at[4:7, 0:16], ext.at[0:3, 0:16], up, has_up, has_down),
        send_to(7, ext.at[4:7, 13:16], ext.at[0:3, 21:24], up | right, has_up & has_right, has_down & has_left),
        send_to(8, ext.at[4:7, 0:3], ext.at[0:3, 16:19], up | left, has_up & has_left, has_down & has_right),
        send_to(9, ext.at[3:6, 13:16], ext.at[7:10, 21:24], down | right, has_down & has_right, has_up & has_left),
        send_to(10, ext.at[3:6, 0:3], ext.at[7:10, 16:19], down | left, has_down & has_left, has_up & has_right),
        send_to(11, ext.at[3:7, 13:16], ext.at[3:7, 21:24], right, has_right, has_left),
        send_to(12, ext.at[3:7, 0:3], ext.at[3:7, 16:19], left, has_left, has_right),
    ]
    for arrived in halo:
        arrived()

    for j in range(4):
        cols = slice(j * CHUNK, (j + 1) * CHUNK)
        layers = filter_z([ext[k, :, cols] for k in range(10)])
        for z in range(4):
            out[z, :, cols] = box_twice(layers[z], 0)[0:16]
    for drained in started:
        drained()


def body(displacements, density, solid, fixed):
    dma = pltpu.SemaphoreType.DMA
    return pl.pallas_call(
        kernel,
        out_shape=jax.ShapeDtypeStruct((4, 16, 512), F32),
        in_specs=[pl.BlockSpec(memory_space=pl.ANY)] * 4,
        out_specs=pl.BlockSpec(memory_space=pltpu.VMEM),
        scratch_shapes=[
            pltpu.VMEM((2, 3, 4, 16, 512), F32),
            pltpu.VMEM((4, 16, 512), F32),
            pltpu.VMEM((4, 16, 512), jnp.int32),
            pltpu.VMEM((4, 16, 512), jnp.int32),
            pltpu.VMEM((6, 5, 24, 512), F32),
            pltpu.VMEM((2, 5, 24, 8, 512), F32),
            pltpu.VMEM((4, 16, 512), F32),
            pltpu.VMEM((4, 16, 512), F32),
            pltpu.VMEM((4, 16, 512), F32),
            pltpu.VMEM((4, 16, 512), F32),
            pltpu.VMEM((10, 24, 512), F32),
            dma((4,)),
            dma((13,)),
            dma((13,)),
            pltpu.SemaphoreType.REGULAR,
        ],
        compiler_params=pltpu.CompilerParams(collective_id=0, has_side_effects=True),
    )(displacements, density, solid, fixed)


def solution(mesh):
    return jax.shard_map(
        body,
        mesh=mesh,
        in_specs=(
            P("load", None, "sz", "sy", None),
            P("sz", "sy", None),
            P("sz", "sy", None),
            P("sz", "sy", None),
        ),
        out_specs=P("sz", "sy", None),
        check_vma=False,
    )
```

```python
import functools

import jax
import jax.numpy as jnp
from jax import lax
from jax.experimental import pallas as pl
from jax.experimental.pallas import tpu as pltpu
from jax.sharding import PartitionSpec as P

MESH = pl.DeviceIdType.MESH
F32 = jnp.float32
LAME = 0.3 / (1.3 * 0.4)
SHEAR = 1.0 / 2.6
CHUNK = 128


def line_weight(coord, count):
    total = None
    for step in range(-3, 4):
        inside = (coord + step >= 0) & (coord + step < count)
        piece = jnp.where(inside, F32(4.0 - abs(step)), F32(0.0))
        total = piece if total is None else total + piece
    return total


def box_twice(value, axis):
    size = value.shape[axis]
    value = value + pltpu.roll(value, size - 1, axis)
    value = value + pltpu.roll(value, size - 2, axis)
    value = value + pltpu.roll(value, 1, axis)
    return value + pltpu.roll(value, 2, axis)


def filter_x(value):
    rows, cols = value.shape
    padded = jnp.concatenate([value, jnp.zeros((rows, 128), F32)], axis=1)
    return box_twice(padded, 1)[:, :cols]


def filter_z(layers):
    pairs = [layers[k] + layers[k + 1] for k in range(9)]
    runs = [pairs[k] + pairs[k + 2] for k in range(7)]
    pairs = [runs[k] + runs[k + 1] for k in range(6)]
    return [pairs[k] + pairs[k + 2] for k in range(4)]


def mode_energy(low, high):
    x, y, z = range(3)
    mode = []
    for k in range(3):
        (ls, lx, ly, lxy), (hs, hx, hy, hxy) = low[k], high[k]
        mode.append(
            dict(
                z=hs - ls, x=hx + lx, y=hy + ly, xy=hxy + lxy,
                xz=hx - lx, yz=hy - ly, xyz=hxy - lxy,
            )
        )
    sq = lambda v: v * v
    a, b, c = mode
    div = sq(a["x"] + b["y"] + c["z"])
    normal = sq(a["x"]) + sq(b["y"]) + sq(c["z"])
    shear = sq(a["y"] + b["x"]) + sq(b["z"] + c["y"]) + sq(a["z"] + c["x"])
    bend = sq(b["xy"] + c["xz"]) + sq(a["xy"] + c["yz"]) + sq(a["xz"] + b["yz"])
    six = (
        sq(a["xy"]) + sq(a["xz"]) + sq(b["xy"]) + sq(b["yz"]) + sq(c["xz"]) + sq(c["yz"])
    )
    twist = sq(a["yz"] + b["xz"]) + sq(a["yz"] + c["xy"]) + sq(b["xz"] + c["xy"])
    last = sq(a["xyz"]) + sq(b["xyz"]) + sq(c["xyz"])
    return div, normal, shear, bend, six, twist, last


def weigh(groups):
    div, normal, shear, bend, six, twist, last = groups
    s = 1.0 / 16.0
    return (
        F32(s * LAME) * div
        + F32(s * 2.0 * SHEAR) * normal
        + F32(s * SHEAR) * (shear + six)
        + F32(s * LAME / 3.0) * bend
        + F32(s * SHEAR / 3.0) * twist
        + F32(s * (LAME + 4.0 * SHEAR) / 9.0) * last
    )


def kernel(
    disp, dens, solid, fixed, out,
    raw, fix, den, sol, faces, energy, coef, mine, theirs, slab,
    load_sem, send, recv, ready,
):
    nsz, nsy, nload = lax.axis_size("sz"), lax.axis_size("sy"), lax.axis_size("load")
    sz, sy, ld = lax.axis_index("sz"), lax.axis_index("sy"), lax.axis_index("load")
    has_up, has_down, has_right, has_left = sz < nsz - 1, sz > 0, sy < nsy - 1, sy > 0
    up, down, right, left = {"sz": sz + 1}, {"sz": sz - 1}, {"sy": sy + 1}, {"sy": sy - 1}
    mate = {"load": lax.rem(ld + 1, nload)}
    low, high = ld == 0, ld == 1
    odd = lax.rem(sz, 2) == 1
    even = jnp.logical_not(odd)

    loads = [
        pltpu.make_async_copy(src, dst, load_sem.at[k])
        for k, (src, dst) in enumerate(
            [(fixed, fix.at[0:4, 0:16])]
            + [(disp.at[:, :, z], raw.at[:, :, z, 0:16]) for z in range(4)]
            + [(dens, den), (solid, sol)]
        )
    ]
    for copy in loads:
        copy.start()
    barrier = pltpu.get_barrier_semaphore()

    def greet(sem, device, when=None):
        if when is None:
            pl.semaphore_signal(sem, inc=1, device_id=device, device_id_type=MESH)
        else:
            pl.when(when)(lambda: greet(sem, device))

    greet(barrier, mate)
    greet(barrier, right, has_right)
    greet(barrier, up, has_up)
    greet(barrier, up | right, has_up & has_right)

    started = []

    def send_to(k, src, dst, device, sends=None, takes=None):
        copy = pltpu.make_async_remote_copy(
            src_ref=src, dst_ref=dst, send_sem=send.at[k], recv_sem=recv.at[k],
            device_id=device, device_id_type=MESH,
        )

        def each(act, when):
            if when is None:
                act()
            else:
                pl.when(when)(act)

        each(copy.start, sends)
        started.append(lambda: each(copy.wait_send, sends))
        return lambda: each(copy.wait_recv, takes)

    loads[0].wait()
    loads[1].wait()
    free = F32(1.0) - fix[0, 0:16, :].astype(F32)
    for case in range(2):
        for k in range(3):
            raw[case, k, 0, 0:16, :] = raw[case, k, 0, 0:16, :] * free

    fix[4] = jnp.zeros((24, 512), jnp.int32)
    one = lambda flag: flag.astype(jnp.int32)
    pl.semaphore_wait(barrier, 1 + one(has_down) + one(has_left) + one(has_down & has_left))
    node_z = [
        send_to(0, raw.at[:, :, 0, 0:16], raw.at[:, :, 4, 0:16], down, has_down, has_up),
    ]
    node_c = [
        send_to(
            1, raw.at[:, :, 0, 0:1], raw.at[:, :, 4, 16:17], down | left,
            has_down & has_left, has_up & has_right,
        )
    ]
    node_y = [
        send_to(2, disp.at[:, :, :, 0:1], raw.at[:, :, 0:4, 16:17], left, has_left, has_right),
        send_to(3, fixed.at[:, 0:1], fix.at[0:4, 16:17], left, has_left, has_right),
    ]

    mine[:, 19:21, :] = jnp.zeros((4, 2, 512), F32)
    theirs[:, 19:21, :] = jnp.zeros((4, 2, 512), F32)

    @pl.when(jnp.logical_not(has_up))
    def _():
        slab[7:10] = jnp.zeros((3, 16, 512), F32)
        raw[:, :, 4] = jnp.zeros((2, 3, 24, 512), F32)

    @pl.when(jnp.logical_not(has_down))
    def _():
        slab[0:3] = jnp.zeros((3, 16, 512), F32)

    @pl.when(jnp.logical_not(has_right))
    def _():
        mine[:, 16:19, :] = jnp.zeros((4, 3, 512), F32)
        theirs[:, 16:19, :] = jnp.zeros((4, 3, 512), F32)
        raw[:, :, :, 16:17, :] = jnp.zeros((2, 3, 5, 1, 512), F32)
        fix[0:4, 16:17, :] = jnp.zeros((4, 1, 512), jnp.int32)

    @pl.when(jnp.logical_not(has_left))
    def _():
        mine[:, 21:24, :] = jnp.zeros((4, 3, 512), F32)
        theirs[:, 21:24, :] = jnp.zeros((4, 3, 512), F32)

    row = lax.broadcasted_iota(jnp.int32, (16, 512), 0)
    lane = lax.broadcasted_iota(jnp.int32, (16, 512), 1)
    area = line_weight(lane, 512) * line_weight(row + sy * 16, nsy * 16)
    last_lane = lax.broadcasted_iota(jnp.int32, (8, 512), 1) == 511

    def next_x(value):
        return jnp.where(last_lane, F32(0.0), pltpu.roll(value, 511, 1))

    def make_faces(half, z):
        r = 8 * half
        free_near = F32(1.0) - fix[z, r : r + 8, :].astype(F32)
        free_far = F32(1.0) - fix[z, r + 1 : r + 9, :].astype(F32)
        for case in range(2):
            for k in range(3):
                near = raw[case, k, z, r : r + 8, :] * free_near
                far = raw[case, k, z, r + 1 : r + 9, :] * free_far
                total, diff = near + far, far - near
                total_x, diff_x = next_x(total), next_x(diff)
                m = 12 * case + 4 * k
                faces[half, z, m] = total_x + total
                faces[half, z, m + 1] = total_x - total
                faces[half, z, m + 2] = diff_x + diff
                faces[half, z, m + 3] = diff_x - diff

    def faces_loop(half, first, last):
        def step(z, carry):
            make_faces(half, z)
            return carry

        lax.fori_loop(first, last, step, 0)

    def energy_loop(half, first, last):
        def step(i, carry):
            z, j = first + i // 4, i % 4
            cols = pl.ds(pl.multiple_of(j * CHUNK, CHUNK), CHUNK)
            groups = None
            for case in range(2):
                sides = [
                    [
                        [faces[half, zz, 12 * case + 4 * k + m, :, cols] for m in range(4)]
                        for k in range(3)
                    ]
                    for zz in (z, z + 1)
                ]
                got = mode_energy(*sides)
                groups = got if groups is None else [p + q for p, q in zip(groups, got)]
            energy[z, 8 * half : 8 * half + 8, cols] = weigh(groups)
            return carry

        lax.fori_loop(0, 4 * (last - first), step, 0)

    def finish_layers(first, last):
        for z in range(first, last):
            mine[z, 0:16, :] = filter_x(energy[z] * coef[z])

    def exchange(k, first, last):
        whole = send_to(k, mine.at[first:last, 0:16], theirs.at[first:last, 0:16], mate)
        if k == 6:
            pl.semaphore_wait(ready, 1)
        return [
            whole,
            send_to(k + 1, mine.at[first:last, 13:16], theirs.at[first:last, 21:24], mate | right, has_right, has_left),
            send_to(k + 2, mine.at[first:last, 0:3], theirs.at[first:last, 16:19], mate | left, has_left, has_right),
            send_to(k + 3, mine.at[first:last, 13:16], mine.at[first:last, 21:24], right, has_right, has_left),
            send_to(k + 4, mine.at[first:last, 0:3], mine.at[first:last, 16:19], left, has_left, has_right),
        ]

    def take(arrivals):
        for arrived in arrivals:
            arrived()

    def filter_y(first, last):
        for z in range(first, last):
            slab[3 + z] = box_twice(mine[z] + theirs[z], 0)[0:16]

    make_faces(0, 0)
    for z in range(1, 4):
        loads[1 + z].wait()
        make_faces(0, z)
    energy_loop(0, 0, 3)
    take(node_y)
    greet(ready, mate)
    faces_loop(1, 0, 4)
    energy_loop(1, 0, 3)
    loads[5].wait()
    loads[6].wait()
    for z in range(4):
        weight = area * line_weight(sz * 4 + z, nsz * 4)
        d = den[z]
        coef[z] = sol[z].astype(F32) * (F32(-3.0) * d * d) / weight
    finish_layers(0, 3)
    most = exchange(6, 0, 3)
    take(node_z)
    faces_loop(0, 4, 5)
    energy_loop(0, 3, 4)
    take(node_c)
    faces_loop(1, 4, 5)
    energy_loop(1, 3, 4)
    finish_layers(3, 4)
    rest = exchange(11, 3, 4)
    take(most)
    filter_y(0, 3)
    halo = [
        send_to(16, slab.at[3:6], slab.at[7:10], down, has_down, has_up),
    ]
    take(rest)
    filter_y(3, 4)
    halo += [
        send_to(17, slab.at[4:7], slab.at[0:3], up | mate, high & odd & has_up, low & even & has_down),
        send_to(5, slab.at[4:7], slab.at[0:3], up, (high | even) & has_up, (high | odd) & has_down),
    ]
    take(halo)
    for j in range(4):
        cols = slice(j * CHUNK, (j + 1) * CHUNK)
        layers = filter_z([slab[k, :, cols] for k in range(10)])
        for z in range(4):
            out[z, :, cols] = layers[z]
    for drained in started:
        drained()


def body(displacements, density, solid, fixed):
    dma = pltpu.SemaphoreType.DMA
    return pl.pallas_call(
        kernel,
        out_shape=pltpu.VMEM((4, 16, 512), F32),
        in_specs=[pl.BlockSpec(memory_space=pl.ANY)] * 4,
        out_specs=pl.BlockSpec(memory_space=pltpu.VMEM),
        scratch_shapes=[
            pltpu.VMEM((2, 3, 5, 24, 512), F32),
            pltpu.VMEM((5, 24, 512), jnp.int32),
            pltpu.VMEM((4, 16, 512), F32),
            pltpu.VMEM((4, 16, 512), jnp.int32),
            pltpu.VMEM((2, 5, 24, 8, 512), F32),
            pltpu.VMEM((4, 16, 512), F32),
            pltpu.VMEM((4, 16, 512), F32),
            pltpu.VMEM((4, 24, 512), F32),
            pltpu.VMEM((4, 24, 512), F32),
            pltpu.VMEM((10, 16, 512), F32),
            dma((7,)),
            dma((18,)),
            dma((18,)),
            pltpu.SemaphoreType.REGULAR,
        ],
        compiler_params=pltpu.CompilerParams(collective_id=0, has_side_effects=True),
    )(displacements, density, solid, fixed)


def solution(mesh):
    return jax.shard_map(
        body,
        mesh=mesh,
        in_specs=(
            P("load", None, "sz", "sy", None),
            P("sz", "sy", None),
            P("sz", "sy", None),
            P("sz", "sy", None),
        ),
        out_specs=P("sz", "sy", None),
        check_vma=False,
    )
```

```python
import functools

import jax
import jax.numpy as jnp
from jax import lax
from jax.experimental import pallas as pl
from jax.experimental.pallas import tpu as pltpu
from jax.sharding import PartitionSpec as P

MESH = pl.DeviceIdType.MESH
F32 = jnp.float32
LAME = 0.3 / (1.3 * 0.4)
SHEAR = 1.0 / 2.6
CHUNK = 128


def line_weight(coord, count):
    total = None
    for step in range(-3, 4):
        inside = (coord + step >= 0) & (coord + step < count)
        piece = jnp.where(inside, F32(4.0 - abs(step)), F32(0.0))
        total = piece if total is None else total + piece
    return total


def box_twice(value, axis):
    size = value.shape[axis]
    value = value + pltpu.roll(value, size - 1, axis)
    value = value + pltpu.roll(value, size - 2, axis)
    value = value + pltpu.roll(value, 1, axis)
    return value + pltpu.roll(value, 2, axis)


def filter_x(value):
    rows, cols = value.shape
    padded = jnp.concatenate([value, jnp.zeros((rows, 128), F32)], axis=1)
    return box_twice(padded, 1)[:, :cols]


def filter_z(layers):
    pairs = [layers[k] + layers[k + 1] for k in range(9)]
    runs = [pairs[k] + pairs[k + 2] for k in range(7)]
    pairs = [runs[k] + runs[k + 1] for k in range(6)]
    return [pairs[k] + pairs[k + 2] for k in range(4)]


def mode_energy(low, high):
    x, y, z = range(3)
    mode = []
    for k in range(3):
        (ls, lx, ly, lxy), (hs, hx, hy, hxy) = low[k], high[k]
        mode.append(
            dict(
                z=hs - ls, x=hx + lx, y=hy + ly, xy=hxy + lxy,
                xz=hx - lx, yz=hy - ly, xyz=hxy - lxy,
            )
        )
    sq = lambda v: v * v
    a, b, c = mode
    div = sq(a["x"] + b["y"] + c["z"])
    normal = sq(a["x"]) + sq(b["y"]) + sq(c["z"])
    shear = sq(a["y"] + b["x"]) + sq(b["z"] + c["y"]) + sq(a["z"] + c["x"])
    bend = sq(b["xy"] + c["xz"]) + sq(a["xy"] + c["yz"]) + sq(a["xz"] + b["yz"])
    six = (
        sq(a["xy"]) + sq(a["xz"]) + sq(b["xy"]) + sq(b["yz"]) + sq(c["xz"]) + sq(c["yz"])
    )
    twist = sq(a["yz"] + b["xz"]) + sq(a["yz"] + c["xy"]) + sq(b["xz"] + c["xy"])
    last = sq(a["xyz"]) + sq(b["xyz"]) + sq(c["xyz"])
    return div, normal, shear, bend, six, twist, last


def weigh(groups):
    div, normal, shear, bend, six, twist, last = groups
    s = 1.0 / 16.0
    return (
        F32(s * LAME) * div
        + F32(s * 2.0 * SHEAR) * normal
        + F32(s * SHEAR) * (shear + six)
        + F32(s * LAME / 3.0) * bend
        + F32(s * SHEAR / 3.0) * twist
        + F32(s * (LAME + 4.0 * SHEAR) / 9.0) * last
    )


def kernel(
    disp, dens, solid, fixed, out,
    raw, fix, den, sol, faces, energy, coef, mine, theirs, slab,
    load_sem, send, recv, ready,
):
    nsz, nsy, nload = lax.axis_size("sz"), lax.axis_size("sy"), lax.axis_size("load")
    sz, sy, ld = lax.axis_index("sz"), lax.axis_index("sy"), lax.axis_index("load")
    has_up, has_down, has_right, has_left = sz < nsz - 1, sz > 0, sy < nsy - 1, sy > 0
    up, down, right, left = {"sz": sz + 1}, {"sz": sz - 1}, {"sy": sy + 1}, {"sy": sy - 1}
    mate = {"load": lax.rem(ld + 1, nload)}
    low, high = ld == 0, ld == 1
    odd = lax.rem(sz, 2) == 1
    even = jnp.logical_not(odd)

    loads = [
        pltpu.make_async_copy(src, dst, load_sem.at[k])
        for k, (src, dst) in enumerate(
            [(fixed, fix.at[0:4, 0:16])]
            + [(disp.at[:, :, z], raw.at[:, :, z, 0:16]) for z in range(4)]
            + [(dens, den), (solid, sol)]
        )
    ]
    for copy in loads:
        copy.start()
    barrier = pltpu.get_barrier_semaphore()

    def greet(sem, device, when=None):
        if when is None:
            pl.semaphore_signal(sem, inc=1, device_id=device, device_id_type=MESH)
        else:
            pl.when(when)(lambda: greet(sem, device))

    greet(barrier, mate)
    greet(barrier, right, has_right)
    greet(barrier, up, has_up)
    greet(barrier, up | right, has_up & has_right)

    started = []

    def send_to(k, src, dst, device, sends=None, takes=None):
        copy = pltpu.make_async_remote_copy(
            src_ref=src, dst_ref=dst, send_sem=send.at[k], recv_sem=recv.at[k],
            device_id=device, device_id_type=MESH,
        )

        def each(act, when):
            if when is None:
                act()
            else:
                pl.when(when)(act)

        each(copy.start, sends)
        started.append(lambda: each(copy.wait_send, sends))
        return lambda: each(copy.wait_recv, takes)

    loads[0].wait()
    loads[1].wait()
    free = F32(1.0) - fix[0, 0:16, :].astype(F32)
    for case in range(2):
        for k in range(3):
            raw[case, k, 0, 0:16, :] = raw[case, k, 0, 0:16, :] * free

    fix[4] = jnp.zeros((24, 512), jnp.int32)
    one = lambda flag: flag.astype(jnp.int32)
    pl.semaphore_wait(barrier, 1 + one(has_down) + one(has_left) + one(has_down & has_left))
    node_z = [
        send_to(0, raw.at[:, :, 0, 0:16], raw.at[:, :, 4, 0:16], down, has_down, has_up),
    ]
    node_c = [
        send_to(
            1, raw.at[:, :, 0, 0:1], raw.at[:, :, 4, 16:17], down | left,
            has_down & has_left, has_up & has_right,
        )
    ]
    node_y = [
        send_to(2, disp.at[:, :, :, 0:1], raw.at[:, :, 0:4, 16:17], left, has_left, has_right),
        send_to(3, fixed.at[:, 0:1], fix.at[0:4, 16:17], left, has_left, has_right),
    ]

    greet(ready, mate)

    mine[:, 19:21, :] = jnp.zeros((4, 2, 512), F32)
    theirs[:, 19:21, :] = jnp.zeros((4, 2, 512), F32)

    @pl.when(jnp.logical_not(has_up))
    def _():
        slab[7:10] = jnp.zeros((3, 16, 512), F32)
        raw[:, :, 4] = jnp.zeros((2, 3, 24, 512), F32)

    @pl.when(jnp.logical_not(has_down))
    def _():
        slab[0:3] = jnp.zeros((3, 16, 512), F32)

    @pl.when(jnp.logical_not(has_right))
    def _():
        mine[:, 16:19, :] = jnp.zeros((4, 3, 512), F32)
        theirs[:, 16:19, :] = jnp.zeros((4, 3, 512), F32)
        raw[:, :, :, 16:17, :] = jnp.zeros((2, 3, 5, 1, 512), F32)
        fix[0:4, 16:17, :] = jnp.zeros((4, 1, 512), jnp.int32)

    @pl.when(jnp.logical_not(has_left))
    def _():
        mine[:, 21:24, :] = jnp.zeros((4, 3, 512), F32)
        theirs[:, 21:24, :] = jnp.zeros((4, 3, 512), F32)

    row = lax.broadcasted_iota(jnp.int32, (16, 512), 0)
    lane = lax.broadcasted_iota(jnp.int32, (16, 512), 1)
    area = line_weight(lane, 512) * line_weight(row + sy * 16, nsy * 16)
    last_lane = lax.broadcasted_iota(jnp.int32, (8, 512), 1) == 511

    def next_x(value):
        return jnp.where(last_lane, F32(0.0), pltpu.roll(value, 511, 1))

    def make_faces(half, z):
        r = 8 * half
        free_near = F32(1.0) - fix[z, r : r + 8, :].astype(F32)
        free_far = F32(1.0) - fix[z, r + 1 : r + 9, :].astype(F32)
        for case in range(2):
            for k in range(3):
                near = raw[case, k, z, r : r + 8, :] * free_near
                far = raw[case, k, z, r + 1 : r + 9, :] * free_far
                total, diff = near + far, far - near
                total_x, diff_x = next_x(total), next_x(diff)
                m = 12 * case + 4 * k
                faces[half, z, m] = total_x + total
                faces[half, z, m + 1] = total_x - total
                faces[half, z, m + 2] = diff_x + diff
                faces[half, z, m + 3] = diff_x - diff

    def faces_loop(half, first, last):
        def step(z, carry):
            make_faces(half, z)
            return carry

        lax.fori_loop(first, last, step, 0)

    def energy_loop(half, first, last):
        def step(i, carry):
            z, j = first + i // 4, i % 4
            cols = pl.ds(pl.multiple_of(j * CHUNK, CHUNK), CHUNK)
            groups = None
            for case in range(2):
                sides = [
                    [
                        [faces[half, zz, 12 * case + 4 * k + m, :, cols] for m in range(4)]
                        for k in range(3)
                    ]
                    for zz in (z, z + 1)
                ]
                got = mode_energy(*sides)
                groups = got if groups is None else [p + q for p, q in zip(groups, got)]
            energy[z, 8 * half : 8 * half + 8, cols] = weigh(groups)
            return carry

        lax.fori_loop(0, 4 * (last - first), step, 0)

    def finish_layers(first, last):
        for z in range(first, last):
            mine[z, 0:16, :] = filter_x(energy[z] * coef[z])

    def exchange(k, first, last):
        whole = send_to(k, mine.at[first:last, 0:16], theirs.at[first:last, 0:16], mate)
        if k == 6:
            pl.semaphore_wait(ready, 1)
        return [
            whole,
            send_to(k + 1, mine.at[first:last, 13:16], theirs.at[first:last, 21:24], mate | right, has_right, has_left),
            send_to(k + 2, mine.at[first:last, 0:3], theirs.at[first:last, 16:19], mate | left, has_left, has_right),
            send_to(k + 3, mine.at[first:last, 13:16], mine.at[first:last, 21:24], right, has_right, has_left),
            send_to(k + 4, mine.at[first:last, 0:3], mine.at[first:last, 16:19], left, has_left, has_right),
        ]

    def take(arrivals):
        for arrived in arrivals:
            arrived()

    def filter_y(first, last):
        for z in range(first, last):
            slab[3 + z] = box_twice(mine[z] + theirs[z], 0)[0:16]

    make_faces(0, 0)
    for z in range(1, 4):
        loads[1 + z].wait()
        make_faces(0, z)
    energy_loop(0, 0, 3)
    take(node_y)
    faces_loop(1, 0, 4)
    energy_loop(1, 0, 3)
    loads[5].wait()
    loads[6].wait()
    for z in range(4):
        weight = area * line_weight(sz * 4 + z, nsz * 4)
        d = den[z]
        coef[z] = sol[z].astype(F32) * (F32(-3.0) * d * d) / weight
    finish_layers(0, 3)
    most = exchange(6, 0, 3)
    take(node_z)
    faces_loop(0, 4, 5)
    energy_loop(0, 3, 4)
    take(node_c)
    faces_loop(1, 4, 5)
    energy_loop(1, 3, 4)
    finish_layers(3, 4)
    rest = exchange(11, 3, 4)
    take(most)
    filter_y(0, 3)
    halo = [
        send_to(16, slab.at[3:6], slab.at[7:10], down, has_down, has_up),
    ]
    take(rest)
    filter_y(3, 4)
    halo += [
        send_to(17, slab.at[4:7], slab.at[0:3], up | mate, high & odd & has_up, low & even & has_down),
        send_to(5, slab.at[4:7], slab.at[0:3], up, (high | even) & has_up, (high | odd) & has_down),
    ]
    take(halo)
    for j in range(4):
        cols = slice(j * CHUNK, (j + 1) * CHUNK)
        layers = filter_z([slab[k, :, cols] for k in range(10)])
        for z in range(4):
            out[z, :, cols] = layers[z]
    for drained in started:
        drained()


def body(displacements, density, solid, fixed):
    dma = pltpu.SemaphoreType.DMA
    return pl.pallas_call(
        kernel,
        out_shape=pltpu.VMEM((4, 16, 512), F32),
        in_specs=[pl.BlockSpec(memory_space=pl.ANY)] * 4,
        out_specs=pl.BlockSpec(memory_space=pltpu.VMEM),
        scratch_shapes=[
            pltpu.VMEM((2, 3, 5, 24, 512), F32),
            pltpu.VMEM((5, 24, 512), jnp.int32),
            pltpu.VMEM((4, 16, 512), F32),
            pltpu.VMEM((4, 16, 512), jnp.int32),
            pltpu.VMEM((2, 5, 24, 8, 512), F32),
            pltpu.VMEM((4, 16, 512), F32),
            pltpu.VMEM((4, 16, 512), F32),
            pltpu.VMEM((4, 24, 512), F32),
            pltpu.VMEM((4, 24, 512), F32),
            pltpu.VMEM((10, 16, 512), F32),
            dma((7,)),
            dma((18,)),
            dma((18,)),
            pltpu.SemaphoreType.REGULAR,
        ],
        compiler_params=pltpu.CompilerParams(collective_id=0, has_side_effects=True),
    )(displacements, density, solid, fixed)


def solution(mesh):
    return jax.shard_map(
        body,
        mesh=mesh,
        in_specs=(
            P("load", None, "sz", "sy", None),
            P("sz", "sy", None),
            P("sz", "sy", None),
            P("sz", "sy", None),
        ),
        out_specs=P("sz", "sy", None),
        check_vma=False,
    )
```
